32 devices in a mesh: groups: 2 (over y), ctx: 4 (over z), head: 2 (over x), sub: 2 (over core).
Axes of the slice: x: 2, y: 2, z: 4, core: 2. Of those that a mesh axis runs over, the one named last changes fastest.
Arguments:
- att_query: bfloat16 [1024, 4096], P(('groups', 'ctx'), ('head', 'sub')), parts along dimension 0, may hold values from -4 to 4
- att_gate: bfloat16 [1024, 4096], P(('groups', 'ctx'), ('head', 'sub')), parts along dimension 0, may hold values from -6 to 6
- att_kv: bfloat16 [1024, 1024], P(('groups', 'ctx')), parts along dimension 0, may hold values from -4 to 4
- residual: bfloat16 [1024, 2048], P(('groups', 'ctx'), ('head', 'sub')), parts along dimension 0, may hold values from -0.19921875 to 0.19921875
- out_weight: bfloat16 [4096, 2048], P(('head', 'sub')), may hold values from -0.5 to 0.5
- norm_gain: float32 [2048], replicated, may hold values from 0.1 to 1.9
- in_weight: bfloat16 [2048, 8192], P(None, ('head', 'sub')), may hold values from -0.125 to 0.125
- beta_weight: bfloat16 [2048, 32], P(None, ('head', 'sub')), may hold values from -0.125 to 0.125
- log_decay: float32 [1024, 32], P(('groups', 'ctx'), ('head', 'sub')), parts along dimension 0, may hold values from -0.7 to 0, as said below
- delta_gain: float32 [128], replicated, may hold values from 0.1 to 1.9
Outputs:
- new_residual: bfloat16 [1024, 2048], P(('groups', 'ctx'), ('head', 'sub')), parts along dimension 0
- delta_out: bfloat16 [1024, 4096], P(('groups', 'ctx'), ('head', 'sub')), parts along dimension 0
The draws below stay inside these ranges and needn't reach their ends.
There are 2 independent parts, one for each index of `groups`. The reference program is written for one: setup_inputs(seed, part) draws one part's arguments, and reference() takes and returns one part's arrays. A program takes and returns all parts, laid end to end along the dimension named above; an argument that names none is the same for every part. Nothing has to cross between parts.
Inputs may be any that keep to these rules, and one draw needn't show every extreme that they name: `log_decay`: negative.
All inputs are finite; a program needn't handle non-finite values.
Results may differ from the reference program's by a relative error of at most 0.035.
Values may be sent and summed in bfloat16 or wider, within the bound.
A program may use at most 64 MiB of HBM per device.

```python
import math
import jax
import jax.numpy as jnp
from jax import lax

D = 2048
HEADS = 16
KV_HEADS = 2
HD = 256
KEY_HEADS = 16
DELTA_VALUE_HEADS = 32
DK = 128
DV = 128
PROMPT_TOKENS = 512
N_CTX = 4


def draw_att_kv(key, part):
    base_key = jax.random.fold_in(key, 11)
    entries = jnp.clip(jax.random.normal(base_key, (PROMPT_TOKENS, KV_HEADS, 2, HD), jnp.float32), -4.0, 4.0)
    return entries.reshape(PROMPT_TOKENS, KV_HEADS * 2 * HD).astype(jnp.bfloat16)


def draw_att_query(key, part):
    base_key = jax.random.fold_in(key, 13)
    entries = jnp.clip(jax.random.normal(base_key, (PROMPT_TOKENS, HEADS, HD), jnp.float32), -4.0, 4.0)
    return entries.reshape(PROMPT_TOKENS, HEADS * HD).astype(jnp.bfloat16)


def draw_log_decay(key, part):
    key_sequence = jax.random.split(jax.random.fold_in(key, 17), 4)
    quick_heads = jax.random.randint(key_sequence[0], (DELTA_VALUE_HEADS,), 0, 10) >= 5
    baseline_rate = jnp.where(quick_heads, -1.0 / 40.0, -math.log(10.0) / (2.0 * PROMPT_TOKENS))
    jaggedness = jnp.exp(jax.random.uniform(key_sequence[1], (PROMPT_TOKENS, DELTA_VALUE_HEADS), jnp.float32, math.log(0.5), math.log(2.0)))
    spike_events = jax.random.randint(key_sequence[2], (PROMPT_TOKENS, DELTA_VALUE_HEADS), 0, PROMPT_TOKENS) < 2
    spike_rate = jnp.log(jax.random.uniform(key_sequence[3], (PROMPT_TOKENS, DELTA_VALUE_HEADS), jnp.float32, 0.5, 0.8))
    gentle_spike = jnp.logical_and(spike_events, jnp.logical_not(quick_heads)[None, :])
    return jnp.where(gentle_spike, spike_rate, baseline_rate[None, :] * jaggedness).astype(jnp.float32)


def raised(values, stream_key, source, target, blocks, factor):
    owner, partner = [(jnp.arange(values.shape[position]) // (values.shape[position] // blocks)).reshape([-1 if axis == position else 1 for axis in range(values.ndim)]) for position in (source, target)]
    chosen = jax.random.permutation(stream_key, blocks)[partner]
    strong = (owner == chosen) | (owner == (partner + blocks // 2) % blocks)
    return jnp.where(strong, factor * values, values)


def steps_of(own_key, extent, cuts, least, top_value):
    level, own = 1.0, jax.random.fold_in(own_key, 6)
    for axis_at, shards_of in cuts:
        heights = jnp.exp(jax.random.uniform(jax.random.fold_in(own, axis_at), (shards_of,), jnp.float32, least / len(cuts), top_value / len(cuts)))
        level = level * jnp.repeat(heights, extent[axis_at] // shards_of).reshape([-1 if axis == axis_at else 1 for axis in range(len(extent))])
    return level


def centred(key, dims, width, bound, cuts=(), held_as=jnp.bfloat16):
    drawn = width * jax.random.normal(key, dims, jnp.float32)
    if cuts:
        drawn = drawn * steps_of(key, dims, cuts, -0.22, 0.18)
    return jnp.clip(drawn, -bound, bound).astype(held_as)


def noise_with(own_key, extent, width, limit, cuts, heavy, kind=jnp.bfloat16):
    array = width * jax.random.normal(own_key, extent, jnp.float32)
    if cuts:
        array = array * steps_of(own_key, extent, cuts, -0.22, 0.18)
    return jnp.clip(raised(array, jax.random.fold_in(own_key, 3), *heavy), -limit, limit).astype(kind)


def setup_inputs(seed: int = 0, part: int = 0) -> dict:
    arg_keys = jax.random.split(jax.random.key(seed), 11)
    part_keys = jax.random.split(jax.random.fold_in(arg_keys[10], part), 11)
    att_query = draw_att_query(jax.random.fold_in(jax.random.fold_in(arg_keys[10], part), 71), part)
    att_gate = centred(part_keys[1], (PROMPT_TOKENS, HEADS * HD), 1.0, 6.0, ((0, 4), (1, 4)))
    att_kv = draw_att_kv(jax.random.fold_in(jax.random.fold_in(arg_keys[10], part), 71), part)
    residual = jnp.clip(jax.random.uniform(part_keys[3], (PROMPT_TOKENS, D), jnp.float32, -0.19921875, 0.19921875) * steps_of(part_keys[3], (PROMPT_TOKENS, D), ((0, 4), (1, 4)), -0.4, 0.0), -0.19921875, 0.19921875).astype(jnp.bfloat16)
    out_weight = noise_with(arg_keys[4], (HEADS * HD, D), HD ** -0.5, 0.5, ((0, 4),), (0, 1, 4, 2.0))
    norm_gain = jnp.clip(1.0 + 0.18 * jax.random.normal(arg_keys[5], (D,), jnp.float32), 0.1, 1.9)
    in_weight = centred(arg_keys[6], (D, KEY_HEADS * (2 * DK + 2 * DV)), D ** -0.5, 0.125, ((1, 4),))
    beta_weight = centred(arg_keys[7], (D, DELTA_VALUE_HEADS), D ** -0.5, 0.125, ((1, 4),))
    log_decay = draw_log_decay(jax.random.fold_in(jax.random.fold_in(arg_keys[10], part), 71), part)
    delta_gain = jnp.clip(1.0 + 0.18 * jax.random.normal(arg_keys[9], (DV,), jnp.float32), 0.1, 1.9)
    return {"att_query": att_query, "att_gate": att_gate, "att_kv": att_kv, "residual": residual, "out_weight": out_weight, "norm_gain": norm_gain, "in_weight": in_weight, "beta_weight": beta_weight, "log_decay": log_decay, "delta_gain": delta_gain}


TOP_PRECISION = lax.Precision.HIGHEST
EPSILON = 1e-06

def stored_positions(total_rows, ctx_devices):
    half_rows = total_rows // (2 * ctx_devices)
    row_index = jnp.arange(total_rows, dtype=jnp.int32)
    device_of = row_index // (2 * half_rows)
    within_dev = row_index % (2 * half_rows)
    block_number = jnp.where(within_dev < half_rows, device_of, 2 * ctx_devices - 1 - device_of)
    return (block_number * half_rows + within_dev % half_rows).astype(jnp.int32)

def unit_rows(matrix):
    return matrix * lax.rsqrt(lax.optimization_barrier(jnp.sum(matrix * matrix, axis=-1, keepdims=True)) + EPSILON)

def reference(att_query, att_gate, att_kv, residual, out_weight, norm_gain, in_weight, beta_weight, log_decay, delta_gain):
    places = stored_positions(PROMPT_TOKENS, N_CTX)
    visible = places[:, None] >= places[None, :]
    group_size = HEADS // KV_HEADS
    score_scale = HD ** (-0.5)

    def one_head(head_number):
        query_rows = lax.dynamic_slice_in_dim(att_query, head_number * HD, HD, 1)
        gate_rows = lax.dynamic_slice_in_dim(att_gate, head_number * HD, HD, 1)
        kv_number = head_number // group_size
        key_rows = lax.dynamic_slice_in_dim(att_kv, kv_number * 2 * HD, HD, 1)
        value_rows = lax.dynamic_slice_in_dim(att_kv, kv_number * 2 * HD + HD, HD, 1)
        scores = jnp.dot(query_rows, key_rows.T, preferred_element_type=jnp.float32) * score_scale
        scores = jnp.where(visible, scores, -1e+30)
        row_max = lax.optimization_barrier(jnp.max(scores, axis=1, keepdims=True))
        weights = jnp.where(visible, jnp.exp(scores - row_max), 0.0)
        denominator = lax.optimization_barrier(jnp.sum(weights, axis=1, keepdims=True))
        attended = jnp.dot(weights.astype(jnp.bfloat16), value_rows, preferred_element_type=jnp.float32) / denominator
        return (attended * jax.nn.sigmoid(gate_rows.astype(jnp.float32))).astype(jnp.bfloat16)
    per_head = lax.map(one_head, jnp.arange(HEADS, dtype=jnp.int32))
    att_heads = jnp.transpose(per_head, (1, 0, 2)).reshape(PROMPT_TOKENS, HEADS * HD)
    hidden = residual.astype(jnp.float32) + jnp.dot(att_heads, out_weight, preferred_element_type=jnp.float32)
    new_residual = hidden.astype(jnp.bfloat16)
    mean_square = lax.optimization_barrier(jnp.mean(hidden * hidden, axis=1, keepdims=True))
    normed = (hidden * lax.rsqrt(mean_square + EPSILON) * norm_gain).astype(jnp.bfloat16)
    projected = jnp.dot(normed, in_weight, preferred_element_type=jnp.float32)
    grouped = projected.reshape(PROMPT_TOKENS, KEY_HEADS, 2 * DK + 2 * DV)
    query_unit = jnp.repeat(unit_rows(jax.nn.silu(grouped[:, :, :DK])) * DK ** (-0.5), 2, axis=1)
    key_unit = jnp.repeat(unit_rows(jax.nn.silu(grouped[:, :, DK:2 * DK])), 2, axis=1)
    value_all = jax.nn.silu(grouped[:, :, 2 * DK:]).reshape(PROMPT_TOKENS, DELTA_VALUE_HEADS, DV)
    beta_rows = jax.nn.sigmoid(jnp.dot(normed, beta_weight, preferred_element_type=jnp.float32))
    natural_order = jnp.argsort(places).astype(jnp.int32)

    def advance(recurrent_state, inputs):
        current_query, current_key, value_now, beta_now, decay_now = inputs
        retention = jnp.exp(decay_now)[:, None]
        retrieved_values = jnp.einsum('ge,gej->gj', current_key, recurrent_state, precision=TOP_PRECISION)
        written = beta_now[:, None] * (value_now - retention * retrieved_values)
        recurrent_state = retention[:, :, None] * recurrent_state + current_key[:, :, None] * written[:, None, :]
        layer_output = jnp.einsum('ge,gej->gj', current_query, recurrent_state, precision=TOP_PRECISION)
        return (recurrent_state, layer_output)
    start_state = jnp.zeros((DELTA_VALUE_HEADS, DK, DV), jnp.float32)
    sequence_inputs = (query_unit[natural_order], key_unit[natural_order], value_all[natural_order], beta_rows[natural_order], log_decay[natural_order])
    final_state, natural_out = lax.scan(advance, start_state, sequence_inputs)
    stored_out = natural_out[places]
    out_square = lax.optimization_barrier(jnp.mean(stored_out * stored_out, axis=2, keepdims=True))
    delta_out = (stored_out * lax.rsqrt(out_square + EPSILON) * delta_gain).astype(jnp.bfloat16)
    return (new_residual, delta_out.reshape(PROMPT_TOKENS, DELTA_VALUE_HEADS * DV))
```

```python
import functools

import jax
import jax.numpy as jnp
from jax import lax
from jax.experimental import pallas as pl
from jax.experimental.pallas import tpu as pltpu
from jax.sharding import PartitionSpec as P

HEADS = 16
KV_HEADS = 2
HD = 256
DK = 128
DV = 128
EPSILON = 1e-06
NEGATIVE = -1e30
PIECES = 2
LATE_FROM = 1
FIRST_STOP = 4
SECOND_STOP = 10
SECOND_TWO = 6
F32 = jnp.float32
BF16 = jnp.bfloat16
MESH = pl.DeviceIdType.MESH


def dot(a, b):
    return jnp.dot(a, b, preferred_element_type=F32)


def dot_nt(a, b):
    return lax.dot_general(a, b, (((1,), (1,)), ((), ())), preferred_element_type=F32)


def dot_tn(a, b):
    return lax.dot_general(a, b, (((0,), (0,)), ((), ())), preferred_element_type=F32)


def silu(x):
    return x * jax.nn.sigmoid(x)


def unit(x):
    return x * lax.rsqrt(jnp.sum(x * x, axis=-1, keepdims=True) + EPSILON)


def remote(src, dst, sems, index, device):
    return pltpu.make_async_remote_copy(
        src_ref=src,
        dst_ref=dst,
        send_sem=sems.at[0, index],
        recv_sem=sems.at[1, index],
        device_id=device,
        device_id_type=MESH,
    )


def kernel(
    ctx_count,
    head_count,
    query_hbm,
    gate_hbm,
    kv_hbm,
    res_hbm,
    ow_hbm,
    norm_gain_hbm,
    iw_hbm,
    bw_hbm,
    ld_hbm,
    delta_gain_hbm,
    new_res_ref,
    delta_ref,
    query_ref,
    gate_ref,
    res_ref,
    norm_gain_ref,
    bw_ref,
    ld_ref,
    delta_gain_ref,
    kv_early,
    kv_late,
    ow,
    iw,
    att,
    rs_send,
    rs_recv,
    x_send,
    x_recv,
    part,
    hid,
    macc,
    grid_ref,
    growth_ref,
    carry_ref,
    whole_ref,
    trans,
    offs,
    early_in,
    late_in,
    early_out,
    late_out,
    local_out,
    read,
    load_sem,
    kv_sem,
    kvf_sem,
    rs_sem,
    x_sem,
    agf_sem,
    early_sem,
    late_sem,
):
    c = lax.axis_index("ctx")
    h = lax.axis_index("head")
    s = lax.axis_index("sub")
    rows = query_ref.shape[0]
    half = rows // 2
    heads_here = query_ref.shape[1] // HD
    width = res_ref.shape[1]
    partner = {"sub": 1 - s}
    kv_number = (h * 2 + s) * heads_here // (HEADS // KV_HEADS)
    last = ctx_count - 1
    group = 2 * DK + 2 * DV
    key_here = iw.shape[1] // group
    value_here = 2 * key_here
    kv_parts = [kv_early, kv_late]
    sends = []

    def block_rows(source):
        return pl.ds(pl.multiple_of(source * half, half), half)

    def half_rows(b):
        return slice(b * half, (b + 1) * half)

    loads = []
    for b in range(2):
        for p in range(2):
            start = pl.multiple_of(kv_number * 2 * HD + p * HD, HD)
            loads.append(
                pltpu.make_async_copy(
                    kv_hbm.at[half_rows(b), pl.ds(start, HD)],
                    kv_parts[b].at[p, block_rows(c)],
                    load_sem.at[b * 2 + p],
                )
            )
    ow_load = pltpu.make_async_copy(ow_hbm, ow, load_sem.at[4])
    iw_load = pltpu.make_async_copy(iw_hbm, iw, load_sem.at[5])
    small = [
        pltpu.make_async_copy(source, target, load_sem.at[6 + i])
        for i, (source, target) in enumerate(
            [
                (query_hbm, query_ref),
                (gate_hbm, gate_ref),
                (res_hbm, res_ref),
                (ld_hbm, ld_ref),
                (norm_gain_hbm, norm_gain_ref),
                (bw_hbm, bw_ref),
                (delta_gain_hbm, delta_gain_ref),
            ]
        )
    ]
    for load in loads + small[:2] + [ow_load] + small[2:]:
        load.start()

    barrier = pltpu.get_barrier_semaphore()
    for d in range(1, ctx_count):
        pl.semaphore_signal(
            barrier, inc=1, device_id={"ctx": lax.rem(c + d, ctx_count)}, device_id_type=MESH
        )
    for d in range(1, head_count):
        pl.semaphore_signal(
            barrier, inc=1, device_id={"head": lax.rem(h + d, head_count)}, device_id_type=MESH
        )
    pl.semaphore_signal(barrier, inc=1, device_id=partner, device_id_type=MESH)

    @pl.when(c == 0)
    def _():
        early_in[...] = jnp.zeros_like(early_in)

    for load in loads:
        load.wait()
    pl.semaphore_wait(barrier, ctx_count + head_count - 1)

    def kv_send(b, d):
        piece = kv_parts[b].at[s, block_rows(c)]
        target = {"ctx": lax.rem(c + d, ctx_count)}
        return remote(piece, piece, kv_sem, b * last + d - 1, target)

    def kv_forward(b, d):
        piece = kv_parts[b].at[s, block_rows(lax.rem(c - d + ctx_count, ctx_count))]
        return remote(piece, piece, kvf_sem, b * last + d - 1, partner)

    for d in range(1, ctx_count):

        @pl.when(c + d < ctx_count)
        def _():
            kv_send(0, d).start()

    for d in range(last, 0, -1):

        @pl.when(c + d >= ctx_count)
        def _():
            kv_send(0, d).start()
            kv_send(1, d).start()

    iw_load.start()
    for load in small:
        load.wait()

    triangle_row = lax.broadcasted_iota(jnp.int32, (half, half), 0)
    triangle_col = lax.broadcasted_iota(jnp.int32, (half, half), 1)
    causal = triangle_row >= triangle_col

    def attend(b, own, keys, values):
        for n in range(heads_here):
            cols = slice(n * HD, (n + 1) * HD)
            query = query_ref[half_rows(b), cols]
            scores = []
            for at, key in zip(own, keys):
                piece = dot_nt(query, key) * (HD**-0.5)
                if at is not None:
                    row = lax.broadcasted_iota(jnp.int32, piece.shape, 0)
                    col = lax.broadcasted_iota(jnp.int32, piece.shape, 1)
                    hidden = (col - at > row) & (col < at + half)
                    piece = jnp.where(hidden, NEGATIVE, piece)
                scores.append(piece)
            top = functools.reduce(
                jnp.maximum, [jnp.max(piece, axis=1, keepdims=True) for piece in scores]
            )
            weights = [jnp.exp(piece - top) for piece in scores]
            total = sum(jnp.sum(piece, axis=1, keepdims=True) for piece in weights)
            mixed = sum(dot(piece.astype(BF16), value) for piece, value in zip(weights, values))
            mixed = mixed / total
            gate = jax.nn.sigmoid(gate_ref[half_rows(b), cols].astype(F32))
            att[half_rows(b), cols] = (mixed * gate).astype(BF16)

    peers = [lax.rem(h + 1 + i, head_count) for i in range(head_count)]

    def shard_of(i, side):
        return peers[i] * 2 + side

    def rs_copy(b, i):
        return remote(rs_send.at[b, i], rs_recv.at[b, i], rs_sem, b * head_count + i, partner)

    def x_copy(b, d, i):
        return remote(
            x_send.at[b, i],
            x_recv.at[b, d - 1, i],
            x_sem,
            (b * max(head_count - 1, 1) + d - 1) * head_count + i,
            {"head": lax.rem(h + d, head_count)},
        )

    def out_projection(b):
        attended = att[half_rows(b), :]

        def out_slice(number):
            return dot(attended, ow[:, pl.ds(pl.multiple_of(number * width, width), width)])

        for i in range(head_count):
            rs_send[b, i] = out_slice(shard_of(i, 1 - s)).astype(BF16)
            rs_copy(b, i).start()
        for i in range(head_count):
            own = out_slice(shard_of(i, s))
            if i == head_count - 1:
                own = own + res_ref[half_rows(b), :].astype(F32)
            rs_copy(b, i).wait_recv()
            own = own + rs_recv[b, i].astype(F32)
            part[b, i] = own
            x_send[b, i] = own.astype(BF16)
            for d in range(1, head_count):
                x_copy(b, d, i).start()

    def hidden_copy(b, i):
        mine = hid.at[b, shard_of(i, s)]
        return remote(mine, mine, agf_sem, b * head_count + i, partner)

    def projection(b):
        for i in range(head_count):
            own = part[b, i]
            for d in range(1, head_count):
                j = (i + d) % head_count
                x_copy(b, d, j).wait_recv()
                own = own + x_recv[b, d - 1, j].astype(F32)
            own16 = own.astype(BF16)
            if i == head_count - 1:
                new_res_ref[half_rows(b), :] = own16
            hid[b, shard_of(i, s)] = own16
            hidden_copy(b, i).start()
            parts = projected(b, shard_of(i, s), parts if i else None)
        for i in range(head_count):
            hidden_copy(b, i).wait_recv()
            parts = projected(b, shard_of(i, 1 - s), parts)
        return parts

    def projected(b, r, start):
        cols = pl.ds(pl.multiple_of(r * width, width), width)
        piece = hid[b, r].astype(F32)
        scaled = (piece * norm_gain_ref[:, cols]).astype(BF16)
        term = dot(scaled, iw[cols, :])
        logits = dot_nt(bw_ref[:, cols], scaled)
        square = jnp.sum(piece * piece, axis=1, keepdims=True)
        if start is None:
            macc[b] = term
            return logits, square
        macc[b] += term
        return start[0] + logits, start[1] + square

    row = lax.broadcasted_iota(jnp.int32, (rows, rows), 0)
    col = lax.broadcasted_iota(jnp.int32, (rows, rows), 1)

    def masks():
        same = (row < half) == (col < half)
        return same, same & (row >= col)

    def twice(values, b, j):
        lines = half_rows(b)
        return jnp.concatenate(
            [values[lines, 2 * j : 2 * j + 1], values[lines, 2 * j + 1 : 2 * j + 2]], axis=0
        )

    def decay_tables():
        same, on_or_below = masks()
        eye = jnp.where(row == col, 1.0, 0.0)
        decays = ld_ref[...]

        def row_sums(picked):
            return lax.dot_general(
                decays,
                jnp.where(picked, 1.0, 0.0),
                (((1,), (1,)), ((), ())),
                precision=lax.Precision.HIGHEST,
                preferred_element_type=F32,
            )

        cumulative = row_sums(on_or_below).T
        block_sum = row_sums(same).T
        rest = jnp.exp(block_sum - cumulative)
        whole = jnp.exp(block_sum)
        for b in range(2):
            for j in range(key_here):
                wide = jnp.broadcast_to(twice(cumulative, b, j), (rows, rows))
                gap = wide - wide.T
                grid_ref[b, j] = jnp.where(
                    on_or_below, jnp.exp(jnp.where(on_or_below, gap, 0.0)), 0.0
                )
                growth_ref[b, j] = jnp.exp(wide)
                carry_ref[b, j] = jnp.broadcast_to(twice(rest, b, j), (rows, rows))
            for n in range(value_here):
                whole_ref[b, n] = whole[b * half : b * half + 1, n : n + 1] * eye[:DK, :DK]

    nxt = {"ctx": lax.min(c + 1, last)}
    prv = {"ctx": lax.max(c - 1, 0)}

    def early_copy(n):
        return remote(early_out.at[n], early_in.at[n], early_sem, n, nxt)

    def late_copy(n):
        return remote(late_out.at[n], late_in.at[n], late_sem, n, prv)

    def piece_rows(p):
        return slice(p * DV // PIECES, (p + 1) * DV // PIECES)

    def delta(b, parts):
        same, on_or_below = masks()
        strictly = same & (row > col)
        eye = jnp.where(row == col, 1.0, 0.0)
        scale = lax.rsqrt(parts[1] / (2 * head_count * width) + EPSILON)
        beta_all = jax.nn.sigmoid(parts[0].T * scale)

        def doubled(x):
            return jnp.concatenate([x, x], axis=0)

        queries, keys, values, betas, systems, inverses, grids = [], [], [], [], [], [], []
        for j in range(key_here):
            m = macc[b, :, j * group : (j + 1) * group] * scale
            q = doubled(unit(silu(m[:, :DK])) * DK**-0.5)
            k = doubled(unit(silu(m[:, DK : 2 * DK])))
            v = silu(m[:, 2 * DK :])
            v = jnp.concatenate([v[:, :DV], v[:, DV:]], axis=0)
            beta = jnp.concatenate(
                [beta_all[:, 2 * j : 2 * j + 1], beta_all[:, 2 * j + 1 : 2 * j + 2]], axis=0
            )
            q16, k16 = q.astype(BF16), k.astype(BF16)
            queries.append(q)
            keys.append(k)
            values.append(v)
            betas.append(beta)
            grid = grid_ref[b, j]
            system = jnp.where(strictly, beta * dot_nt(k16, k16) * grid, 0.0)
            grids.append((dot_nt(q16, k16) * grid).astype(BF16))
            systems.append(system)
            inverses.append(eye - jnp.where((row >> 1) == (col >> 1), system, 0.0))
        level = 1
        while (1 << level) < half:
            mask = ((row >> (level + 1)) == (col >> (level + 1))) & (
                (row >> level) != (col >> level)
            )
            halves = [inverse.astype(BF16) for inverse in inverses]
            firsts = [
                dot(jnp.where(mask, system, 0.0).astype(BF16), inverse).astype(BF16)
                for system, inverse in zip(systems, halves)
            ]
            inverses = [
                full - dot(inverse, product)
                for full, inverse, product in zip(inverses, halves, firsts)
            ]
            level += 1
        solutions = []
        for j in range(key_here):
            right = jnp.concatenate(
                [betas[j] * values[j], betas[j] * growth_ref[b, j] * keys[j]], axis=1
            )
            solutions.append(dot(inverses[j].astype(BF16), right.astype(BF16)).astype(BF16))
        for j in range(key_here):
            carried = (keys[j] * carry_ref[b, j]).astype(BF16)
            for i in range(2):
                n = 2 * j + i
                lines = half_rows(i)
                ends = dot_tn(solutions[j][lines], carried[lines])
                offs[b, n] = ends[:DV]
                trans[b, n] = (whole_ref[b, n] - ends[DV:]).astype(BF16)
                if b == 0:
                    for p in range(PIECES):
                        early_out[n * PIECES + p] = ends[piece_rows(p)].astype(BF16)
            if b == 0:

                @pl.when(c == 0)
                def _():
                    for at in range(2 * j * PIECES, 2 * (j + 1) * PIECES):
                        early_copy(at).start()

        for j in range(key_here):
            inner = dot(grids[j], solutions[j])
            local_out[b, j] = inner[:, :DV]
            read[b, j] = (growth_ref[b, j] * queries[j] - inner[:, DV:]).astype(BF16)

    def passed(n, p, b, state):
        return (dot(state, trans[b, n]) + offs[b, n, piece_rows(p), :]).astype(BF16)

    def early_relay(low, high):
        def early_turn(at, carried):
            n = at // PIECES
            early_copy(at).wait_recv()
            lines = pl.ds(pl.multiple_of(lax.rem(at, PIECES) * (DV // PIECES), DV // PIECES), DV // PIECES)
            end = (dot(early_in[at], trans[0, n]) + offs[0, n, lines, :]).astype(BF16)

            @pl.when(c < last)
            def _():
                early_out[at] = end
                early_copy(at).start()

            @pl.when(c == last)
            def _():
                late_in[at] = end
                late_out[at] = (dot(end, trans[1, n]) + offs[1, n, lines, :]).astype(BF16)
                late_copy(at).start()

            return carried

        lax.fori_loop(low, high, early_turn, 0)

    def finish(n, b, state):
        pair, side = n // 2, n % 2
        if isinstance(n, int):
            lines = half_rows(side)
        else:
            lines = pl.ds(pl.multiple_of(lax.rem(n, 2) * half, half), half)
        out = local_out[b, pair, lines, :] + dot_nt(read[b, pair, lines, :], state)
        mean = jnp.mean(out * out, axis=1, keepdims=True)
        out = out * lax.rsqrt(mean + EPSILON) * delta_gain_ref[...]
        if isinstance(n, int):
            delta_ref[half_rows(b), n * DV : (n + 1) * DV] = out.astype(BF16)
        else:
            delta_ref[half_rows(b), pl.ds(pl.multiple_of(n * DV, DV), DV)] = out.astype(BF16)

    def whole_state(ref, n):
        return jnp.concatenate([ref[n * PIECES + p] for p in range(PIECES)], axis=0)

    for d in range(1, ctx_count):

        @pl.when(c >= d)
        def _():
            kv_send(0, d).wait_recv()
            kv_forward(0, d).start()

    for d in range(1, ctx_count):

        @pl.when(c >= d)
        def _():
            kv_forward(0, d).wait_recv()

    for k in range(ctx_count):

        @pl.when(c == k)
        def _():
            lines = slice(0, (k + 1) * half)
            attend(0, [k * half], [kv_early[0, lines]], [kv_early[1, lines]])

    ow_load.wait()
    out_projection(0)
    decay_tables()

    def late_front(choices):
        for d in range(last, 0, -1):

            @pl.when(c < d)
            def _():
                for b in range(2):
                    kv_send(b, d).wait_recv()
                    kv_forward(b, d).start()

        for d in range(last, 0, -1):

            @pl.when(c < d)
            def _():
                for b in range(2):
                    kv_forward(b, d).wait_recv()

        for k in choices:

            @pl.when(c == k)
            def _():
                lines = slice(k * half, ctx_count * half)
                attend(
                    1,
                    [None, 0],
                    [kv_early[0], kv_late[0, lines]],
                    [kv_early[1], kv_late[1, lines]],
                )

        out_projection(1)

    @pl.when(c >= LATE_FROM)
    def _():
        late_front(range(LATE_FROM, ctx_count))

    iw_load.wait()
    delta(0, projection(0))

    @pl.when(c < LATE_FROM)
    def _():
        late_front(range(LATE_FROM))

    pieces = value_here * PIECES
    first_stop = jnp.where(c == 1, FIRST_STOP * pieces // 16, 0)
    second_stop = jnp.where(c == 1, SECOND_STOP * pieces // 16, jnp.where(c == 2, SECOND_TWO * pieces // 16, 0))
    third_stop = jnp.where(c > 0, pieces, 0)
    early_relay(0, first_stop)
    late_parts = projection(1)
    early_relay(first_stop, second_stop)
    delta(1, late_parts)
    early_relay(second_stop, third_stop)

    for n in range(value_here):
        finish(n, 0, whole_state(early_in, n))

    @pl.when((c > 0) & (c < last))
    def _():
        def late_turn(n, carried):
            for p in range(PIECES):
                at = n * PIECES + p
                late_copy(at).wait_recv()
                late_out[at] = passed(n, p, 1, late_in[at])
                late_copy(at).start()
            return carried

        lax.fori_loop(0, value_here, late_turn, 0)

    @pl.when(c == 0)
    def _():
        def last_turn(n, carried):
            for p in range(PIECES):
                late_copy(n * PIECES + p).wait_recv()
            finish(n, 1, whole_state(late_in, n))
            return carried

        lax.fori_loop(0, value_here, last_turn, 0)

    @pl.when(c > 0)
    def _():
        for n in range(value_here):
            finish(n, 1, whole_state(late_in, n))

    for d in range(1, ctx_count):
        kv_send(0, d).wait_send()
        kv_forward(0, d).wait_send()

        @pl.when(c + d >= ctx_count)
        def _():
            kv_send(1, d).wait_send()

        @pl.when(c < d)
        def _():
            kv_forward(1, d).wait_send()

    for b in range(2):
        for i in range(head_count):
            rs_copy(b, i).wait_send()
            hidden_copy(b, i).wait_send()
            for d in range(1, head_count):
                x_copy(b, d, i).wait_send()

    def drain(n, carry):
        @pl.when(c < last)
        def _():
            early_copy(n).wait_send()

        @pl.when(c > 0)
        def _():
            late_copy(n).wait_send()

        return carry

    lax.fori_loop(0, value_here * PIECES, drain, 0)


def settle(first_ref, second_ref, first_out, second_out):
    first_out[...] = first_ref[...]
    second_out[...] = second_ref[...]


def local(
    ctx_count,
    head_count,
    att_query,
    att_gate,
    att_kv,
    residual,
    out_weight,
    norm_gain,
    in_weight,
    beta_weight,
    log_decay,
    delta_gain,
):
    rows = att_query.shape[0]
    width = residual.shape[1]
    value_here = log_decay.shape[1]
    vmem = pl.BlockSpec(memory_space=pltpu.VMEM)
    hbm = pl.BlockSpec(memory_space=pl.ANY)
    heads_less = max(head_count - 1, 1)
    pair = pltpu.SemaphoreType.DMA
    outputs = pl.pallas_call(
        functools.partial(kernel, ctx_count, head_count),
        out_shape=(
            jax.ShapeDtypeStruct((rows, width), BF16),
            jax.ShapeDtypeStruct((rows, value_here * DV), BF16),
        ),
        in_specs=[hbm] * 10,
        out_specs=(vmem, vmem),
        scratch_shapes=[
            pltpu.VMEM(att_query.shape, BF16),
            pltpu.VMEM(att_gate.shape, BF16),
            pltpu.VMEM(residual.shape, BF16),
            pltpu.VMEM((1, norm_gain.shape[0]), F32),
            pltpu.VMEM(beta_weight.shape[::-1], BF16),
            pltpu.VMEM(log_decay.shape[::-1], F32),
            pltpu.VMEM((1, DV), F32),
            pltpu.VMEM((2, ctx_count * rows // 2, HD), BF16),
            pltpu.VMEM((2, ctx_count * rows // 2, HD), BF16),
            pltpu.VMEM(out_weight.shape, BF16),
            pltpu.VMEM(in_weight.shape, BF16),
            pltpu.VMEM(att_query.shape, BF16),
            pltpu.VMEM((2, head_count, rows // 2, width), BF16),
            pltpu.VMEM((2, head_count, rows // 2, width), BF16),
            pltpu.VMEM((2, head_count, rows // 2, width), BF16),
            pltpu.VMEM((2, heads_less, head_count, rows // 2, width), BF16),
            pltpu.VMEM((2, head_count, rows // 2, width), F32),
            pltpu.VMEM((2, 2 * head_count, rows // 2, width), BF16),
            pltpu.VMEM((2, rows // 2, in_weight.shape[1]), F32),
            pltpu.VMEM((2, value_here // 2, rows, rows), F32),
            pltpu.VMEM((2, value_here // 2, rows, rows), F32),
            pltpu.VMEM((2, value_here // 2, rows, rows), F32),
            pltpu.VMEM((2, value_here, DK, DK), F32),
            pltpu.VMEM((2, value_here, DK, DK), BF16),
            pltpu.VMEM((2, value_here, DV, DK), F32),
            pltpu.VMEM((value_here * PIECES, DV // PIECES, DK), BF16),
            pltpu.VMEM((value_here * PIECES, DV // PIECES, DK), BF16),
            pltpu.VMEM((value_here * PIECES, DV // PIECES, DK), BF16),
            pltpu.VMEM((value_here * PIECES, DV // PIECES, DK), BF16),
            pltpu.VMEM((2, value_here // 2, rows, DV), F32),
            pltpu.VMEM((2, value_here // 2, rows, DK), BF16),
            pair((13,)),
            pair((2, 2 * (ctx_count - 1))),
            pair((2, 2 * (ctx_count - 1))),
            pair((2, 2 * head_count)),
            pair((2, 2 * heads_less * head_count)),
            pair((2, 2 * head_count)),
            pair((2, value_here * PIECES)),
            pair((2, value_here * PIECES)),
        ],
        compiler_params=pltpu.CompilerParams(collective_id=0, has_side_effects=True),
    )(
        att_query,
        att_gate,
        att_kv,
        residual,
        out_weight,
        norm_gain.reshape(1, -1),
        in_weight,
        beta_weight.T,
        log_decay.T,
        delta_gain.reshape(1, -1),
    )
    return pl.pallas_call(
        settle,
        out_shape=tuple(jax.ShapeDtypeStruct(x.shape, x.dtype) for x in outputs),
        in_specs=[vmem, vmem],
        out_specs=(vmem, vmem),
    )(*outputs)


def solution(mesh):
    return jax.shard_map(
        functools.partial(local, mesh.shape["ctx"], mesh.shape["head"]),
        mesh=mesh,
        in_specs=(
            P(("groups", "ctx"), ("head", "sub")),
            P(("groups", "ctx"), ("head", "sub")),
            P(("groups", "ctx"), None),
            P(("groups", "ctx"), ("head", "sub")),
            P(("head", "sub"), None),
            P(),
            P(None, ("head", "sub")),
            P(None, ("head", "sub")),
            P(("groups", "ctx"), ("head", "sub")),
            P(),
        ),
        out_specs=(P(("groups", "ctx"), ("head", "sub")), P(("groups", "ctx"), ("head", "sub"))),
        check_vma=False,
    )
```
